256 devices in a mesh: user: 16 (over x, y_hi, core), item: 16 (over z, y_lo).
Axes of the slice: x: 4, y: 4 (y_hi: 2, y_lo: 2; y = y_hi * 2 + y_lo), z: 8, core: 2. Of those that a mesh axis runs over, the one named last changes fastest.
Arguments:
- item_factors: float32 [16, 4096, 128], P('item', 'user'), may hold values from -2 to 2
- weights: float32 [128, 256, 128, 128], P('user', 'item'), may hold values from 0 to 100
- tile_ids: int32 [128, 16, 16], P('user', 'item'), may hold values from 0 to 31, as said below
- start_factors: float32 [16384, 128], P('user'), may hold values from -4 to 4
Outputs:
- user_factors: float32 [16384, 128], P('user')
The draws below stay inside these ranges and needn't reach their ends.
Inputs may be any that keep to these rules, and one draw needn't show every extreme that they name: `tile_ids`: entries of one user block and item block are distinct.
All inputs are finite; a program needn't handle non-finite values.
Results may differ from the reference program's by a relative error of at most 0.0003.
Values sent between devices are 32-bit elements; how exact they have to be, the bound alone decides.
A program may use at most 64 MiB of HBM per device.

```python
import jax
import jax.numpy as jnp
from jax import lax

R = 128
TILE = 128
NT = 32
K = 16
UB = 8
ITERS = 3
UBLOCKS = 128
USERS = 16384
N_USER = 16
N_ITEM = 16


def draw_item_factors(key, part):
    keys = jax.random.split(jax.random.fold_in(key, 11), 3)
    rows = N_ITEM * NT * TILE
    normal = jax.random.normal(keys[0], (rows, R), jnp.float32)
    colscale = jnp.exp(jax.random.uniform(keys[1], (1, R), jnp.float32, jnp.log(0.3), jnp.log(3.0)))
    ramp = 0.6 + 1.2 * jnp.arange(rows, dtype=jnp.float32)[:, None] / rows
    rough = jax.random.uniform(keys[2], (rows, 1), jnp.float32, 0.5, 1.5)
    base = normal
    values = 0.03 * base * colscale * ramp * rough
    return jnp.clip(values, -2.0, 2.0).reshape(N_ITEM, NT * TILE, R)


def draw_weights(key, part):
    keys = jax.random.split(jax.random.fold_in(key, 23), 6)
    ublocks = UB * N_USER
    kall = K * N_ITEM
    shape = (ublocks, kall, TILE, TILE)
    density = jnp.exp(jax.random.uniform(keys[0], (ublocks, kall, TILE, 1), jnp.float32, jnp.log(0.02), jnp.log(0.95)))
    observed = jax.random.uniform(keys[1], shape, jnp.float32) < density
    tile_level = jnp.exp(jax.random.uniform(keys[2], (ublocks, kall, TILE, 1), jnp.float32, 0.0, jnp.log(5.0)))
    region = jnp.exp(jax.random.uniform(keys[3], (ublocks, N_ITEM, 1, TILE, 1), jnp.float32, 0.0, jnp.log(10.0)))
    region = jnp.broadcast_to(region, (ublocks, N_ITEM, K, TILE, 1)).reshape(ublocks, kall, TILE, 1)
    entry = jnp.exp(jax.random.uniform(keys[5], shape, jnp.float32, 0.0, jnp.log(2.0)))
    values = jnp.minimum(entry * tile_level * region, 100.0)
    return jnp.where(observed, values, 0.0)


def draw_tile_ids(key, part):
    scores = jax.random.randint(jax.random.fold_in(key, 37), (UB * N_USER, N_ITEM, NT), 0, 1 << 20)
    scores = scores * NT + jnp.arange(NT, dtype=jnp.int32)
    return lax_top(scores)


def lax_top(scores):
    return jax.lax.top_k(scores, K)[1].astype(jnp.int32)


def block_levels(own_key, dims, cuts, smallest, top_value):
    loudness = 1.0
    for axis_at, blocks in cuts:
        heights = jax.random.uniform(jax.random.fold_in(jax.random.fold_in(own_key, 6), axis_at), (blocks,), jnp.float32, smallest / len(cuts), top_value / len(cuts))
        loudness = loudness * jnp.repeat(jnp.exp(heights), dims[axis_at] // blocks).reshape((-1,) + (1,) * (len(dims) - 1 - axis_at))
    return loudness


def centred(stream_key, shape, width, reach, cuts=(), kind=jnp.bfloat16):
    entries = width * jax.random.normal(stream_key, shape, jnp.float32)
    if cuts:
        entries = entries * block_levels(stream_key, shape, cuts, -0.22, 0.18)
    return jnp.clip(entries, -reach, reach).astype(kind)


def setup_inputs(seed: int = 0) -> dict:
    arg_keys = jax.random.split(jax.random.key(seed), 5)
    item_factors = draw_item_factors(jax.random.fold_in(arg_keys[4], 71), 0)
    weights = draw_weights(jax.random.fold_in(arg_keys[4], 71), 0)
    tile_ids = draw_tile_ids(jax.random.fold_in(arg_keys[4], 71), 0)
    start_factors = centred(arg_keys[3], (USERS, R), 0.5, 4.0, ((0, 16),), jnp.float32)
    return {"item_factors": item_factors, "weights": weights, "tile_ids": tile_ids, "start_factors": start_factors}


HIGH = lax.Precision.HIGHEST


def reference(item_factors, weights, tile_ids, start_factors):
    factors = item_factors.reshape(-1, R)
    gram = jnp.dot(factors.T, factors, preferred_element_type=jnp.float32, precision=HIGH)
    vtiles = factors.reshape(N_ITEM, NT, TILE, R)
    wblocks = weights.reshape(UBLOCKS, N_ITEM * K, TILE, TILE)
    starts = start_factors.reshape(UBLOCKS, TILE, R)
    blocks_idx = jnp.arange(N_ITEM, dtype=jnp.int32)[:, None]

    def one_block(args):
        wblock, idblock, start = args
        chosen = vtiles[blocks_idx, idblock.astype(jnp.int32)].reshape(N_ITEM * K, TILE, R)

        def apply(vec):
            scores = jnp.einsum("kjr,ur->kuj", chosen, vec, precision=HIGH)
            back = jnp.einsum("kuj,kjr->ur", scores * wblock, chosen, precision=HIGH)
            return back + jnp.dot(vec, gram, preferred_element_type=jnp.float32, precision=HIGH) + 1.0 * vec

        prefs = jnp.where(wblock > 0, 1.0 + wblock, 0.0)
        rhs = jnp.einsum("kuj,kjr->ur", prefs, chosen, precision=HIGH)
        solved = start
        resid = rhs - apply(solved)
        direction = resid
        norm_now = jnp.sum(resid * resid, axis=1, keepdims=True)
        for step in range(ITERS):
            image = apply(direction)
            alpha = norm_now / (jnp.sum(direction * image, axis=1, keepdims=True) + 1e-6)
            solved = solved + alpha * direction
            resid = resid - alpha * image
            norm_next = jnp.sum(resid * resid, axis=1, keepdims=True)
            direction = resid + (norm_next / (norm_now + 1e-6)) * direction
            norm_now = norm_next
        return solved

    result = lax.map(one_block, (wblocks, tile_ids, starts))
    return result.reshape(USERS, R)
```

```python
import functools

import jax
import jax.numpy as jnp
from jax import lax
from jax.experimental import pallas as pl
from jax.experimental.pallas import tpu as pltpu
from jax.sharding import PartitionSpec as P

F32 = jnp.float32
BF16 = jnp.bfloat16
MESH = pl.DeviceIdType.MESH

ITERS = 3
ROUNDS = ITERS + 1
PERIOD = 12
AT_SUM = 2
AT_SOLVE = 6
AT_SPREAD = 10

NX, NYH, NCORE = 4, 2, 2
NZ, NYL = 8, 2


def split(value):
    high = value.astype(BF16)
    low = (value - high.astype(F32)).astype(BF16)
    return high, low


def kernel(
    blocks,
    count,
    ids_ref,
    weights_hbm,
    slab_ref,
    start_hbm,
    out_hbm,
    weights_ref,
    vbuf,
    vcat,
    gram_acc,
    gram_cat,
    direct,
    part,
    ybuf,
    zsum,
    zbuf,
    xs,
    rs,
    ps,
    norms,
    local_sem,
    out_sem,
    g_send,
    g_recv,
    y_send,
    y_recv,
    z_send,
    z_recv,
    a_send,
    a_recv,
    b_send,
    b_recv,
):
    user = lax.axis_index("user")
    item = lax.axis_index("item")
    tile = direct.shape[1]
    half = tile // NYL
    piece = half // NZ
    rows = slab_ref.shape[0]

    load_w = pltpu.make_async_copy(weights_hbm, weights_ref, local_sem.at[0])
    load_w.start()
    load_x = pltpu.make_async_copy(start_hbm, direct, local_sem.at[1])
    load_x.start()

    px, pyh, pc = user // (NYH * NCORE), lax.rem(user // NCORE, NYH), lax.rem(user, NCORE)
    pz, pyl = item // NYL, lax.rem(item, NYL)

    def uslot(x, yh, c):
        return x * (NYH * NCORE) + yh * NCORE + c

    xl, xr, xo = lax.rem(px + 3, NX), lax.rem(px + 1, NX), lax.rem(px + 2, NX)
    qyh, qc = 1 - pyh, 1 - pc
    dev_y = (uslot(px, qyh, pc), item)
    dev_l = (uslot(xl, pyh, pc), item)
    dev_r = (uslot(xr, pyh, pc), item)
    dev_c = (uslot(px, pyh, qc), item)
    dev_p = (user, pz * NYL + (1 - pyl))

    def dev_z(rel):
        return (user, lax.rem(pz + rel, NZ) * NYL + pyl)

    barrier = pltpu.get_barrier_semaphore()
    greeted = [dev_y, dev_l, dev_r, dev_c, dev_p] + [dev_z(rel) for rel in range(1, NZ)]
    for dev in greeted:
        pl.semaphore_signal(barrier, inc=1, device_id=dev, device_id_type=MESH)
    pl.semaphore_wait(barrier, len(greeted))

    sends = []

    def send(src, slot, lo, n, dev, sem):
        copy = pltpu.make_async_remote_copy(
            src_ref=src.at[pl.ds(lo, n)],
            dst_ref=vbuf.at[slot, pl.ds(lo, n)],
            send_sem=g_send.at[sem],
            recv_sem=g_recv.at[sem],
            device_id=dev,
            device_id_type=MESH,
        )
        copy.start()
        sends.append(copy)

    def arrived(slot, lo, n, sem):
        view = vbuf.at[slot, pl.ds(lo, n)]
        pltpu.make_async_copy(view, view, g_recv.at[sem]).wait()

    gram_acc[...] = jnp.zeros_like(gram_acc)

    def convert(src, slot):
        for j in range(rows // tile):
            high, low = split(src[pl.ds(j * tile, tile), :])
            cat = jnp.concatenate([high, low], axis=1)
            vcat[slot * (rows // tile) + j] = cat
            gram_acc[...] += lax.dot_general(
                cat, cat, (((0,), (0,)), ((), ())), preferred_element_type=F32
            )

    own = uslot(px, pyh, pc)
    HB = rows // 2
    Y, L0, R0, L1, R1, O0A, O0B, O1A, O1B, C0 = 0, 1, 2, 3, 4, 5, 6, 7, 8, 9
    send(slab_ref, own, 0, rows, dev_y, Y)
    send(slab_ref, own, 0, rows, dev_r, L0)
    send(slab_ref, own, 0, rows, dev_l, R0)
    send(slab_ref, own, 0, rows, dev_c, C0)
    convert(slab_ref, own)

    def take(slot, sem, right, left, core):
        arrived(slot, 0, rows, sem)
        if right is not None:
            send(vbuf.at[slot], slot, 0, right[1], dev_r, right[0])
        if left is not None:
            send(vbuf.at[slot], slot, rows - left[1], left[1], dev_l, left[0])
        send(vbuf.at[slot], slot, 0, rows, dev_c, core)

    take(uslot(xl, pyh, pc), L0, (O0A, HB), None, C0 + 2)
    take(uslot(xr, pyh, pc), R0, None, (O0B, HB), C0 + 3)
    convert(vbuf.at[uslot(xl, pyh, pc)], uslot(xl, pyh, pc))
    take(uslot(px, qyh, pc), Y, (L1, rows), (R1, rows), C0 + 1)
    convert(vbuf.at[uslot(xr, pyh, pc)], uslot(xr, pyh, pc))
    convert(vbuf.at[uslot(px, qyh, pc)], uslot(px, qyh, pc))
    near = uslot(xo, pyh, pc)
    arrived(near, 0, HB, O0A)
    arrived(near, HB, HB, O0B)
    send(vbuf.at[near], near, 0, rows, dev_c, C0 + 6)
    convert(vbuf.at[near], near)
    take(uslot(xl, qyh, pc), L1, (O1A, HB), None, C0 + 4)
    take(uslot(xr, qyh, pc), R1, None, (O1B, HB), C0 + 5)
    convert(vbuf.at[uslot(xl, qyh, pc)], uslot(xl, qyh, pc))
    convert(vbuf.at[uslot(xr, qyh, pc)], uslot(xr, qyh, pc))
    cores = [
        (uslot(px, pyh, qc), C0),
        (uslot(xl, pyh, qc), C0 + 2),
        (uslot(xr, pyh, qc), C0 + 3),
        (uslot(px, qyh, qc), C0 + 1),
        (uslot(xo, pyh, qc), C0 + 6),
        (uslot(xl, qyh, qc), C0 + 4),
        (uslot(xr, qyh, qc), C0 + 5),
    ]
    for slot, sem in cores[:5]:
        arrived(slot, 0, rows, sem)
        convert(vbuf.at[slot], slot)
    far = uslot(xo, qyh, pc)
    arrived(far, 0, HB, O1A)
    arrived(far, HB, HB, O1B)
    send(vbuf.at[far], far, 0, rows, dev_c, C0 + 7)
    convert(vbuf.at[far], far)
    for slot, sem in cores[5:] + [(uslot(xo, qyh, qc), C0 + 7)]:
        arrived(slot, 0, rows, sem)
        convert(vbuf.at[slot], slot)
    for copy in sends:
        copy.wait_send()

    gram = gram_acc[...]
    gram = gram[:tile] + gram[tile:]
    gram = gram[:, :tile] + gram[:, tile:]
    gram_cat[...] = jnp.concatenate(split(gram), axis=1)

    load_x.wait()
    load_w.wait()

    def image(c, first):
        vec = direct[c]
        if first:
            vec = -vec
        high, low = split(vec)
        lhs = jnp.concatenate(
            [jnp.concatenate([high, high], axis=1), jnp.concatenate([low, low], axis=1)], axis=0
        )
        acc = jnp.dot(
            jnp.concatenate([high, low], axis=0), gram_cat[...], preferred_element_type=F32
        )
        for k in range(0, count, 2):
            base = c * count + k
            pair = jnp.concatenate([vcat[ids_ref[base]], vcat[ids_ref[base + 1]]], axis=0)
            scores = lax.dot_general(
                lhs, pair, (((1,), (1,)), ((), ())), preferred_element_type=F32
            )
            scores = scores[:tile] + scores[tile:]
            wt = jnp.concatenate([weights_ref[base], weights_ref[base + 1]], axis=1)
            scaled = scores * wt
            if first:
                scaled = scaled + jnp.where(wt > 0, 1.0 + wt, 0.0)
            acc += jnp.dot(
                jnp.concatenate(split(scaled), axis=0), pair, preferred_element_type=F32
            )
        acc = acc[:tile] + acc[tile:]
        part[c] = acc[:, :tile] + acc[:, tile:]

    mine = pl.multiple_of(pyl * half, half)
    other = pl.multiple_of((1 - pyl) * half, half)
    zrow = pl.multiple_of(pz * piece, piece)
    prow = pl.multiple_of(pyl * half + pz * piece, piece)

    def copy_y(c):
        return pltpu.make_async_remote_copy(
            src_ref=part.at[c, pl.ds(other, half)],
            dst_ref=ybuf.at[c],
            send_sem=y_send.at[c],
            recv_sem=y_recv.at[c],
            device_id=dev_p,
            device_id_type=MESH,
        )

    def copy_b(c):
        return pltpu.make_async_remote_copy(
            src_ref=direct.at[c, pl.ds(mine, half)],
            dst_ref=direct.at[c, pl.ds(mine, half)],
            send_sem=b_send.at[c],
            recv_sem=b_recv.at[c],
            device_id=dev_p,
            device_id_type=MESH,
        )

    def wait_all(c, sem):
        view = zbuf.at[c]
        pltpu.make_async_copy(view, view, sem.at[c]).wait()

    def stage_image(c, t):
        @pl.when(t > 0)
        def _():
            copy_b(c).wait()

        @pl.when(t == 0)
        def _():
            image(c, True)

        @pl.when(jnp.logical_and(t > 0, t < ROUNDS))
        def _():
            image(c, False)

        @pl.when(t < ROUNDS)
        def _():
            copy_y(c).start()

        @pl.when(t == ROUNDS)
        def _():
            pltpu.make_async_copy(direct.at[c], out_hbm.at[c], out_sem.at[c]).start()

    def stage_sum(c):
        copy_y(c).wait()
        zsum[c] = part[c, pl.ds(mine, half), :] + ybuf[c]
        for rel in range(1, NZ):
            row = pl.multiple_of(lax.rem(pz + rel, NZ) * piece, piece)
            pltpu.make_async_remote_copy(
                src_ref=zsum.at[c, pl.ds(row, piece)],
                dst_ref=zbuf.at[c, NZ - 1 - rel],
                send_sem=z_send.at[c],
                recv_sem=z_recv.at[c],
                device_id=dev_z(rel),
                device_id_type=MESH,
            ).start()

    def spread(c):
        for rel in range(1, NZ):
            pltpu.make_async_remote_copy(
                src_ref=direct.at[c, pl.ds(prow, piece)],
                dst_ref=direct.at[c, pl.ds(prow, piece)],
                send_sem=a_send.at[c],
                recv_sem=a_recv.at[c],
                device_id=dev_z(rel),
                device_id_type=MESH,
            ).start()

    def stage_solve(c, t):
        wait_all(c, z_send)
        wait_all(c, z_recv)
        got = zsum[c, pl.ds(zrow, piece), :]
        for k in range(NZ - 1):
            got = got + zbuf[c, k]

        @pl.when(t == 0)
        def _():
            x0 = direct[c, pl.ds(prow, piece), :]
            r = got - 1.0 * x0
            xs[c] = x0
            rs[c] = r
            ps[c] = r
            norms[c] = jnp.broadcast_to(jnp.sum(r * r, axis=1, keepdims=True), r.shape)
            direct[c, pl.ds(prow, piece), :] = r

        @pl.when(t > 0)
        def _():
            p = ps[c]
            q = got + 1.0 * p
            now = norms[c]
            alpha = now / (jnp.sum(p * q, axis=1, keepdims=True) + 1e-06)
            x = xs[c] + alpha * p
            r = rs[c] - alpha * q
            after = jnp.broadcast_to(jnp.sum(r * r, axis=1, keepdims=True), r.shape)
            p = r + after / (now + 1e-06) * p
            xs[c] = x
            rs[c] = r
            ps[c] = p
            norms[c] = after
            direct[c, pl.ds(prow, piece), :] = jnp.where(t == ROUNDS - 1, x, p)

        spread(c)

    def stage_spread(c):
        wait_all(c, a_send)
        wait_all(c, a_recv)
        copy_b(c).start()

    def guarded(step, offset, rounds, body):
        at = step - offset
        t = lax.div(at, PERIOD)
        c = lax.rem(at, PERIOD)

        @pl.when(jnp.logical_and(at >= 0, jnp.logical_and(t < rounds, c < blocks)))
        def _():
            body(c, t)

    def step_body(step, carry):
        guarded(step, AT_SPREAD, ROUNDS, lambda c, t: stage_spread(c))
        guarded(step, AT_SOLVE, ROUNDS, stage_solve)
        guarded(step, AT_SUM, ROUNDS, lambda c, t: stage_sum(c))
        guarded(step, 0, ROUNDS + 1, stage_image)
        return carry

    lax.fori_loop(0, ROUNDS * PERIOD + blocks, step_body, 0)
    for c in range(blocks):
        pltpu.make_async_copy(direct.at[c], out_hbm.at[c], out_sem.at[c]).wait()


def local(item_factors, weights, tile_ids, start_factors):
    blocks, count, tile, _ = weights.shape
    _, rows, rank = item_factors.shape
    gathered = NX * NYH * NCORE
    half = tile // NYL
    piece = half // NZ
    dma = pltpu.SemaphoreType.DMA
    vmem = pltpu.VMEM
    out = pl.pallas_call(
        functools.partial(kernel, blocks, count),
        out_shape=jax.ShapeDtypeStruct((blocks, tile, rank), F32),
        in_specs=[
            pl.BlockSpec(memory_space=pltpu.SMEM),
            pl.BlockSpec(memory_space=pl.ANY),
            pl.BlockSpec(memory_space=vmem),
            pl.BlockSpec(memory_space=pl.ANY),
        ],
        out_specs=pl.BlockSpec(memory_space=pl.ANY),
        scratch_shapes=[
            vmem((blocks * count, tile, tile), F32),
            vmem((gathered, rows, rank), F32),
            vmem((gathered * rows // tile, tile, 2 * rank), BF16),
            vmem((2 * rank, 2 * rank), F32),
            vmem((rank, 2 * rank), BF16),
            vmem((blocks, tile, rank), F32),
            vmem((blocks, tile, rank), F32),
            vmem((blocks, half, rank), F32),
            vmem((blocks, half, rank), F32),
            vmem((blocks, NZ - 1, piece, rank), F32),
            vmem((blocks, piece, rank), F32),
            vmem((blocks, piece, rank), F32),
            vmem((blocks, piece, rank), F32),
            vmem((blocks, piece, rank), F32),
            dma((2,)),
            dma((blocks,)),
            dma((17,)),
            dma((17,)),
        ]
        + [dma((blocks,))] * 8,
        compiler_params=pltpu.CompilerParams(collective_id=0, has_side_effects=True),
        name="als_sweep",
    )(
        tile_ids.reshape(blocks * count),
        weights.reshape(blocks * count, tile, tile),
        item_factors.reshape(rows, rank),
        start_factors.reshape(blocks, tile, rank),
    )
    return out.reshape(blocks * tile, rank)


def solution(mesh):
    in_specs = (
        P("item", "user", None),
        P("user", "item", None, None),
        P("user", "item", None),
        P("user", None),
    )
    out_specs = P("user", None)
    return jax.shard_map(local, mesh=mesh, in_specs=in_specs, out_specs=out_specs, check_vma=False)
```

```python
import functools

import jax
import jax.numpy as jnp
from jax import lax
from jax.experimental import pallas as pl
from jax.experimental.pallas import tpu as pltpu
from jax.sharding import PartitionSpec as P

F32 = jnp.float32
BF16 = jnp.bfloat16
MESH = pl.DeviceIdType.MESH

ITERS = 3
ROUNDS = ITERS + 1
PERIOD = 11
AT_SUM = 2
AT_SOLVE = 5
AT_SPREAD = 8
RS_ALL = False
AG_ALL = False

NX, NYH, NCORE = 4, 2, 2
NZ, NYL = 8, 2


def split(value):
    high = value.astype(BF16)
    low = (value - high.astype(F32)).astype(BF16)
    return high, low


def kernel(
    blocks,
    count,
    ids_ref,
    weights_hbm,
    slab_ref,
    start_hbm,
    out_hbm,
    weights_ref,
    vbuf,
    vcat,
    gram_acc,
    gram_cat,
    direct,
    part,
    ybuf,
    zsum,
    zbuf,
    xs,
    rs,
    ps,
    norms,
    local_sem,
    out_sem,
    g_send,
    g_recv,
    y_send,
    y_recv,
    z_send,
    z_recv,
    a_send,
    a_recv,
    b_send,
    b_recv,
):
    user = lax.axis_index("user")
    item = lax.axis_index("item")
    tile = direct.shape[1]
    half = tile // NYL
    piece = half // NZ
    rows = slab_ref.shape[0]

    load_w = pltpu.make_async_copy(weights_hbm, weights_ref, local_sem.at[0])
    load_w.start()
    load_x = pltpu.make_async_copy(start_hbm, direct, local_sem.at[1])
    load_x.start()

    px, pyh, pc = user // (NYH * NCORE), lax.rem(user // NCORE, NYH), lax.rem(user, NCORE)
    pz, pyl = item // NYL, lax.rem(item, NYL)

    def uslot(x, yh, c):
        return x * (NYH * NCORE) + yh * NCORE + c

    xl, xr, xo = lax.rem(px + 3, NX), lax.rem(px + 1, NX), lax.rem(px + 2, NX)
    qyh, qc = 1 - pyh, 1 - pc
    dev_y = (uslot(px, qyh, pc), item)
    dev_l = (uslot(xl, pyh, pc), item)
    dev_r = (uslot(xr, pyh, pc), item)
    dev_o = (uslot(xo, pyh, pc), item)
    dev_c = (uslot(px, pyh, qc), item)
    dev_p = (user, pz * NYL + (1 - pyl))

    peers = [(dz, dy) for dz in (4, 3, 5, 2, 6, 1, 7, 0) for dy in (1, 0) if dz or dy]
    column = [(dz, dy) for dz, dy in peers if dy == 0]
    rs_peers = peers if RS_ALL else column
    ag_peers = peers if AG_ALL else column

    def place(dz, dy):
        return lax.rem(pz + dz, NZ), lax.rem(pyl + dy, NYL)

    def dev_z(dz, dy):
        z, y = place(dz, dy)
        return (user, z * NYL + y)

    def slot_of(dz, dy, group):
        return group.index(((NZ - dz) % NZ, dy))

    barrier = pltpu.get_barrier_semaphore()
    greeted = [dev_y, dev_l, dev_r, dev_o, dev_c] + [dev_z(dz, dy) for dz, dy in peers]
    for dev in greeted:
        pl.semaphore_signal(barrier, inc=1, device_id=dev, device_id_type=MESH)
    pl.semaphore_wait(barrier, len(greeted))

    parts = rows // tile
    sends = []

    def send(src, slot, j, dev, kind):
        copy = pltpu.make_async_remote_copy(
            src_ref=src.at[pl.ds(j * tile, tile)],
            dst_ref=vbuf.at[slot, pl.ds(j * tile, tile)],
            send_sem=g_send.at[kind * parts + j],
            recv_sem=g_recv.at[kind * parts + j],
            device_id=dev,
            device_id_type=MESH,
        )
        copy.start()
        sends.append(copy)

    def arrived(slot, j, kind):
        view = vbuf.at[slot, pl.ds(j * tile, tile)]
        pltpu.make_async_copy(view, view, g_recv.at[kind * parts + j]).wait()

    gram_acc[...] = jnp.zeros_like(gram_acc)

    def convert(src, slot, j):
        high, low = split(src[pl.ds(j * tile, tile), :])
        cat = jnp.concatenate([high, low], axis=1)
        vcat[slot * parts + j] = cat
        gram_acc[...] += lax.dot_general(
            cat, cat, (((0,), (0,)), ((), ())), preferred_element_type=F32
        )

    own = uslot(px, pyh, pc)
    Y, L0, R0, O0, L1, R1, O1, C0 = range(8)
    for j in range(parts):
        send(slab_ref, own, j, dev_y, Y)
        send(slab_ref, own, j, dev_r, L0)
        send(slab_ref, own, j, dev_l, R0)
        send(slab_ref, own, j, dev_o, O0)
        send(slab_ref, own, j, dev_c, C0)
    for j in range(parts):
        convert(slab_ref, own, j)
    across = uslot(px, qyh, pc)
    for j in range(parts):
        arrived(across, j, Y)
        send(vbuf.at[across], across, j, dev_r, L1)
        send(vbuf.at[across], across, j, dev_l, R1)
        send(vbuf.at[across], across, j, dev_o, O1)
        send(vbuf.at[across], across, j, dev_c, C0 + Y + 1)
    routes = [(xl, pyh, L0), (xr, pyh, R0), (xo, pyh, O0), (xl, qyh, L1), (xr, qyh, R1), (xo, qyh, O1)]
    for x, yh, kind in routes[:3]:
        for j in range(parts):
            slot = uslot(x, yh, pc)
            arrived(slot, j, kind)
            send(vbuf.at[slot], slot, j, dev_c, C0 + kind + 1)
    for x, yh, kind in [(px, qyh, Y)] + routes[:3]:
        for j in range(parts):
            convert(vbuf.at[uslot(x, yh, pc)], uslot(x, yh, pc), j)
    for x, yh, kind in [(px, pyh, -1), (px, qyh, Y)] + routes[:3]:
        for j in range(parts):
            slot = uslot(x, yh, qc)
            arrived(slot, j, C0 + kind + 1)
            convert(vbuf.at[slot], slot, j)
    for j in range(parts):
        for x, yh, kind in routes[3:]:
            slot = uslot(x, yh, pc)
            arrived(slot, j, kind)
            send(vbuf.at[slot], slot, j, dev_c, C0 + kind + 1)
            convert(vbuf.at[slot], slot, j)
    for j in range(parts):
        for x, yh, kind in routes[3:]:
            slot = uslot(x, yh, qc)
            arrived(slot, j, C0 + kind + 1)
            convert(vbuf.at[slot], slot, j)
    for copy in sends:
        copy.wait_send()

    gram = gram_acc[...]
    gram = gram[:tile] + gram[tile:]
    gram = gram[:, :tile] + gram[:, tile:]
    gram_cat[...] = jnp.concatenate(split(gram), axis=1)

    load_x.wait()
    load_w.wait()

    def image(c, first):
        vec = direct[c]
        if first:
            vec = -vec
        high, low = split(vec)
        lhs = jnp.concatenate(
            [jnp.concatenate([high, high], axis=1), jnp.concatenate([low, low], axis=1)], axis=0
        )
        acc = jnp.dot(
            jnp.concatenate([high, low], axis=0), gram_cat[...], preferred_element_type=F32
        )
        for k in range(0, count, 2):
            base = c * count + k
            pair = jnp.concatenate([vcat[ids_ref[c, 0, k]], vcat[ids_ref[c, 0, k + 1]]], axis=0)
            scores = lax.dot_general(
                lhs, pair, (((1,), (1,)), ((), ())), preferred_element_type=F32
            )
            scores = scores[:tile] + scores[tile:]
            wt = jnp.concatenate([weights_ref[base], weights_ref[base + 1]], axis=1)
            scaled = scores * wt
            if first:
                scaled = scaled + jnp.where(wt > 0, 1.0 + wt, 0.0)
            acc += jnp.dot(
                jnp.concatenate(split(scaled), axis=0), pair, preferred_element_type=F32
            )
        acc = acc[:tile] + acc[tile:]
        part[c] = acc[:, :tile] + acc[:, tile:]

    mine = pl.multiple_of(pyl * half, half)
    other = pl.multiple_of((1 - pyl) * half, half)
    zrow = pl.multiple_of(pz * piece, piece)
    prow = pl.multiple_of(pyl * half + pz * piece, piece)

    def copy_y(c):
        return pltpu.make_async_remote_copy(
            src_ref=part.at[c, pl.ds(other, half)],
            dst_ref=ybuf.at[c],
            send_sem=y_send.at[c],
            recv_sem=y_recv.at[c],
            device_id=dev_p,
            device_id_type=MESH,
        )

    def copy_b(c):
        return pltpu.make_async_remote_copy(
            src_ref=direct.at[c, pl.ds(mine, half)],
            dst_ref=direct.at[c, pl.ds(mine, half)],
            send_sem=b_send.at[c],
            recv_sem=b_recv.at[c],
            device_id=dev_p,
            device_id_type=MESH,
        )

    def wait_all(c, sem, n):
        view = zbuf.at[c, pl.ds(0, n)]
        pltpu.make_async_copy(view, view, sem.at[c]).wait()

    def scatter(src, c):
        for dz, dy in rs_peers:
            z, y = place(dz, dy)
            row = z * piece + (y * half if RS_ALL else 0)
            pltpu.make_async_remote_copy(
                src_ref=src.at[c, pl.ds(pl.multiple_of(row, piece), piece)],
                dst_ref=zbuf.at[c, slot_of(dz, dy, rs_peers)],
                send_sem=z_send.at[c],
                recv_sem=z_recv.at[c],
                device_id=dev_z(dz, dy),
                device_id_type=MESH,
            ).start()

    def stage_image(c, t):
        @pl.when(t > 0)
        def _():
            if AG_ALL:
                wait_all(c, a_send, len(ag_peers))
                wait_all(c, a_recv, len(ag_peers))
            else:
                copy_b(c).wait()

        @pl.when(t == 0)
        def _():
            image(c, True)

        @pl.when(jnp.logical_and(t > 0, t < ROUNDS))
        def _():
            image(c, False)

        @pl.when(t < ROUNDS)
        def _():
            if RS_ALL:
                scatter(part, c)
            else:
                copy_y(c).start()

        @pl.when(t == ROUNDS)
        def _():
            pltpu.make_async_copy(direct.at[c], out_hbm.at[c], out_sem.at[c]).start()

    def stage_sum(c):
        copy_y(c).wait()
        zsum[c] = part[c, pl.ds(mine, half), :] + ybuf[c]
        scatter(zsum, c)

    def spread(c):
        for dz, dy in ag_peers:
            pltpu.make_async_remote_copy(
                src_ref=direct.at[c, pl.ds(prow, piece)],
                dst_ref=direct.at[c, pl.ds(prow, piece)],
                send_sem=a_send.at[c],
                recv_sem=a_recv.at[c],
                device_id=dev_z(dz, dy),
                device_id_type=MESH,
            ).start()

    def stage_solve(c, t):
        wait_all(c, z_send, len(rs_peers))
        wait_all(c, z_recv, len(rs_peers))
        got = part[c, pl.ds(prow, piece), :] if RS_ALL else zsum[c, pl.ds(zrow, piece), :]
        for k in range(len(rs_peers)):
            got = got + zbuf[c, k]

        @pl.when(t == 0)
        def _():
            x0 = direct[c, pl.ds(prow, piece), :]
            r = got - 1.0 * x0
            xs[c] = x0
            rs[c] = r
            ps[c] = r
            norms[c] = jnp.broadcast_to(jnp.sum(r * r, axis=1, keepdims=True), r.shape)
            direct[c, pl.ds(prow, piece), :] = r

        @pl.when(t > 0)
        def _():
            p = ps[c]
            q = got + 1.0 * p
            now = norms[c]
            alpha = now / (jnp.sum(p * q, axis=1, keepdims=True) + 1e-06)
            x = xs[c] + alpha * p
            r = rs[c] - alpha * q
            after = jnp.broadcast_to(jnp.sum(r * r, axis=1, keepdims=True), r.shape)
            p = r + after / (now + 1e-06) * p
            xs[c] = x
            rs[c] = r
            ps[c] = p
            norms[c] = after
            direct[c, pl.ds(prow, piece), :] = jnp.where(t == ROUNDS - 1, x, p)

        spread(c)

    def stage_spread(c):
        wait_all(c, a_send, len(ag_peers))
        wait_all(c, a_recv, len(ag_peers))
        copy_b(c).start()

    def guarded(step, offset, rounds, body):
        at = step - offset
        t = lax.div(at, PERIOD)
        c = lax.rem(at, PERIOD)

        @pl.when(jnp.logical_and(at >= 0, jnp.logical_and(t < rounds, c < blocks)))
        def _():
            body(c, t)

    def step_body(step, carry):
        guarded(step, 0, ROUNDS + 1, stage_image)
        if not RS_ALL:
            guarded(step, AT_SUM, ROUNDS, lambda c, t: stage_sum(c))
        guarded(step, AT_SOLVE, ROUNDS, stage_solve)
        if not AG_ALL:
            guarded(step, AT_SPREAD, ROUNDS, lambda c, t: stage_spread(c))
        return carry

    lax.fori_loop(0, ROUNDS * PERIOD + blocks, step_body, 0)
    for c in range(blocks):
        pltpu.make_async_copy(direct.at[c], out_hbm.at[c], out_sem.at[c]).wait()


def local(item_factors, weights, tile_ids, start_factors):
    blocks, count, tile, _ = weights.shape
    _, rows, rank = item_factors.shape
    gathered = NX * NYH * NCORE
    half = tile // NYL
    piece = half // NZ
    dma = pltpu.SemaphoreType.DMA
    vmem = pltpu.VMEM
    out = pl.pallas_call(
        functools.partial(kernel, blocks, count),
        out_shape=jax.ShapeDtypeStruct((blocks, tile, rank), F32),
        in_specs=[
            pl.BlockSpec(memory_space=pltpu.SMEM),
            pl.BlockSpec(memory_space=pl.ANY),
            pl.BlockSpec(memory_space=vmem),
            pl.BlockSpec(memory_space=pl.ANY),
        ],
        out_specs=pl.BlockSpec(memory_space=pl.ANY),
        scratch_shapes=[
            vmem((blocks * count, tile, tile), F32),
            vmem((gathered, rows, rank), F32),
            vmem((gathered * rows // tile, tile, 2 * rank), BF16),
            vmem((2 * rank, 2 * rank), F32),
            vmem((rank, 2 * rank), BF16),
            vmem((blocks, tile, rank), F32),
            vmem((blocks, tile, rank), F32),
            vmem((blocks, half, rank), F32),
            vmem((blocks, half, rank), F32),
            vmem((blocks, NZ * NYL - 1, piece, rank), F32),
            vmem((blocks, piece, rank), F32),
            vmem((blocks, piece, rank), F32),
            vmem((blocks, piece, rank), F32),
            vmem((blocks, piece, rank), F32),
            dma((2,)),
            dma((blocks,)),
            dma((15 * rows // tile,)),
            dma((15 * rows // tile,)),
        ]
        + [dma((blocks,))] * 8,
        compiler_params=pltpu.CompilerParams(collective_id=0, has_side_effects=True),
        name="als_sweep",
    )(
        tile_ids,
        weights.reshape(blocks * count, tile, tile),
        item_factors.reshape(rows, rank),
        start_factors.reshape(blocks, tile, rank),
    )
    return out.reshape(blocks * tile, rank)


def solution(mesh):
    in_specs = (
        P("item", "user", None),
        P("user", "item", None, None),
        P("user", "item", None),
        P("user", None),
    )
    out_specs = P("user", None)
    return jax.shard_map(local, mesh=mesh, in_specs=in_specs, out_specs=out_specs, check_vma=False)
```

```python
import functools

import jax
import jax.numpy as jnp
from jax import lax
from jax.experimental import pallas as pl
from jax.experimental.pallas import tpu as pltpu
from jax.sharding import PartitionSpec as P

F32 = jnp.float32
BF16 = jnp.bfloat16
MESH = pl.DeviceIdType.MESH

ITERS = 3
ROUNDS = ITERS
PERIOD = 11
AT_SUM = 2
AT_SOLVE = 5
AT_SPREAD = 8
AT_LAST = 6

NX, NYH, NCORE = 4, 2, 2
NZ, NYL = 8, 2


def split(value):
    high = value.astype(BF16)
    low = (value - high.astype(F32)).astype(BF16)
    return high, low


def kernel(
    blocks,
    count,
    ids_hbm,
    weights_hbm,
    slab_hbm,
    start_hbm,
    out_hbm,
    ids_ref,
    weights_ref,
    vbuf,
    vcat,
    gram_acc,
    gram_cat,
    direct,
    part,
    ybuf,
    zsum,
    zbuf,
    scal,
    dots,
    rs,
    ps,
    norms,
    alphas,
    local_sem,
    out_sem,
    g_send,
    g_recv,
    y_send,
    y_recv,
    z_send,
    z_recv,
    a_send,
    a_recv,
    b_send,
    b_recv,
    s_send,
    s_recv,
    e_send,
    e_recv,
    d_send,
    d_recv,
):
    user = lax.axis_index("user")
    item = lax.axis_index("item")
    tile = direct.shape[2]
    half = tile // NYL
    piece = half // NZ
    rows = vbuf.shape[1]

    px, pyh, pc = user // (NYH * NCORE), lax.rem(user // NCORE, NYH), lax.rem(user, NCORE)
    pz, pyl = item // NYL, lax.rem(item, NYL)

    def uslot(x, yh, c):
        return x * (NYH * NCORE) + yh * NCORE + c

    xl, xr, xo = lax.rem(px + 3, NX), lax.rem(px + 1, NX), lax.rem(px + 2, NX)
    qyh, qc = 1 - pyh, 1 - pc
    dev_y = (uslot(px, qyh, pc), item)
    dev_l = (uslot(xl, pyh, pc), item)
    dev_r = (uslot(xr, pyh, pc), item)
    dev_o = (uslot(xo, pyh, pc), item)
    dev_c = (uslot(px, pyh, qc), item)
    dev_p = (user, pz * NYL + (1 - pyl))

    peers = [(dz, dy) for dz in (4, 3, 5, 2, 6, 1, 7, 0) for dy in (1, 0) if dz or dy]
    column = [(dz, dy) for dz, dy in peers if dy == 0]

    def place(dz, dy):
        return lax.rem(pz + dz, NZ), lax.rem(pyl + dy, NYL)

    def dev_z(dz, dy):
        z, y = place(dz, dy)
        return (user, z * NYL + y)

    def slot_of(dz):
        return column.index((NZ - dz, 0))

    barrier = pltpu.get_barrier_semaphore()
    greeted = [dev_y, dev_l, dev_r, dev_o, dev_c] + [dev_z(dz, dy) for dz, dy in peers]
    for dev in greeted:
        pl.semaphore_signal(barrier, inc=1, device_id=dev, device_id_type=MESH)
    own = uslot(px, pyh, pc)
    load_v = pltpu.make_async_copy(slab_hbm, vbuf.at[own], local_sem.at[2])
    load_v.start()
    load_i = pltpu.make_async_copy(ids_hbm, ids_ref, local_sem.at[3])
    load_i.start()
    load_x = pltpu.make_async_copy(start_hbm, direct.at[0], local_sem.at[1])
    load_x.start()
    load_w = pltpu.make_async_copy(weights_hbm, weights_ref, local_sem.at[0])
    load_w.start()
    load_v.wait()
    pl.semaphore_wait(barrier, len(greeted))

    parts = rows // tile
    sends = []

    def send(src, slot, j, dev, kind):
        copy = pltpu.make_async_remote_copy(
            src_ref=src.at[pl.ds(j * tile, tile)],
            dst_ref=vbuf.at[slot, pl.ds(j * tile, tile)],
            send_sem=g_send.at[kind * parts + j],
            recv_sem=g_recv.at[kind * parts + j],
            device_id=dev,
            device_id_type=MESH,
        )
        copy.start()
        sends.append(copy)

    def arrived(slot, j, kind):
        view = vbuf.at[slot, pl.ds(j * tile, tile)]
        pltpu.make_async_copy(view, view, g_recv.at[kind * parts + j]).wait()

    gram_acc[...] = jnp.zeros_like(gram_acc)

    def convert(src, slot, j):
        high, low = split(src[pl.ds(j * tile, tile), :])
        cat = jnp.concatenate([high, low], axis=1)
        vcat[slot * parts + j] = cat
        gram_acc[...] += lax.dot_general(
            cat, cat, (((0,), (0,)), ((), ())), preferred_element_type=F32
        )

    Y, L0, R0, O0, L1, R1, O1, C0 = range(8)
    for j in range(parts):
        send(vbuf.at[own], own, j, dev_y, Y)
        send(vbuf.at[own], own, j, dev_r, L0)
        send(vbuf.at[own], own, j, dev_l, R0)
        send(vbuf.at[own], own, j, dev_o, O0)
        send(vbuf.at[own], own, j, dev_c, C0)
    for j in range(parts):
        convert(vbuf.at[own], own, j)
    across = uslot(px, qyh, pc)
    for j in range(parts):
        arrived(across, j, Y)
        send(vbuf.at[across], across, j, dev_r, L1)
        send(vbuf.at[across], across, j, dev_l, R1)
        send(vbuf.at[across], across, j, dev_o, O1)
        send(vbuf.at[across], across, j, dev_c, C0 + Y + 1)
    routes = [(xl, pyh, L0), (xr, pyh, R0), (xo, pyh, O0), (xl, qyh, L1), (xr, qyh, R1), (xo, qyh, O1)]
    for x, yh, kind in routes[:3]:
        for j in range(parts):
            slot = uslot(x, yh, pc)
            arrived(slot, j, kind)
            send(vbuf.at[slot], slot, j, dev_c, C0 + kind + 1)
    for x, yh, kind in [(px, qyh, Y)] + routes[:3]:
        for j in range(parts):
            convert(vbuf.at[uslot(x, yh, pc)], uslot(x, yh, pc), j)
    for x, yh, kind in [(px, pyh, -1), (px, qyh, Y)] + routes[:3]:
        for j in range(parts):
            slot = uslot(x, yh, qc)
            arrived(slot, j, C0 + kind + 1)
            convert(vbuf.at[slot], slot, j)
    for j in range(parts):
        for x, yh, kind in routes[3:]:
            slot = uslot(x, yh, pc)
            arrived(slot, j, kind)
            send(vbuf.at[slot], slot, j, dev_c, C0 + kind + 1)
            convert(vbuf.at[slot], slot, j)
    for j in range(parts):
        for x, yh, kind in routes[3:]:
            slot = uslot(x, yh, qc)
            arrived(slot, j, C0 + kind + 1)
            convert(vbuf.at[slot], slot, j)
    for copy in sends:
        copy.wait_send()

    gram = gram_acc[...]
    gram = gram[:tile] + gram[tile:]
    gram = gram[:, :tile] + gram[:, tile:]
    gram_cat[...] = jnp.concatenate(split(gram), axis=1)

    load_i.wait()
    load_x.wait()
    load_w.wait()

    def operand(vec):
        high, low = split(vec)
        lhs = jnp.concatenate(
            [jnp.concatenate([high, high], axis=1), jnp.concatenate([low, low], axis=1)], axis=0
        )
        own_part = jnp.dot(
            jnp.concatenate([high, low], axis=0), gram_cat[...], preferred_element_type=F32
        )
        return lhs, own_part

    def fold(acc):
        acc = acc[:tile] + acc[tile:]
        return acc[:, :tile] + acc[:, tile:]

    def scored(lhs, c, k):
        pair = jnp.concatenate([vcat[ids_ref[c, 0, k]], vcat[ids_ref[c, 0, k + 1]]], axis=0)
        scores = lax.dot_general(lhs, pair, (((1,), (1,)), ((), ())), preferred_element_type=F32)
        base = c * count + k
        wt = jnp.concatenate([weights_ref[base], weights_ref[base + 1]], axis=1)
        return pair, scores[:tile] + scores[tile:], wt

    def image(c, t, first):
        vec = direct[t, c]
        lhs, acc = operand(-vec if first else vec)
        for k in range(0, count, 2):
            pair, scores, wt = scored(lhs, c, k)
            scaled = scores * wt
            if first:
                scaled = scaled + jnp.where(wt > 0, 1.0 + wt, 0.0)
            acc += jnp.dot(
                jnp.concatenate(split(scaled), axis=0), pair, preferred_element_type=F32
            )
        part[c] = fold(acc)

    diagonal = lax.broadcasted_iota(jnp.int32, (tile, tile), 0) == lax.broadcasted_iota(
        jnp.int32, (tile, tile), 1
    )

    def curvature(c):
        vec = direct[ROUNDS, c]
        lhs, own_part = operand(vec)
        acc = None
        for k in range(0, count, 2):
            _, scores, wt = scored(lhs, c, k)
            term = scores * scores * wt
            acc = term if acc is None else acc + term
        share = acc[:, :tile] + acc[:, tile:] + vec * fold(own_part)
        share = jnp.sum(share, axis=1, keepdims=True)
        dots[c, item] = jnp.sum(jnp.where(diagonal, share, 0.0), axis=0, keepdims=True)

    mine = pl.multiple_of(pyl * half, half)
    other = pl.multiple_of((1 - pyl) * half, half)
    zrow = pl.multiple_of(pz * piece, piece)
    prow = pl.multiple_of(pyl * half + pz * piece, piece)

    def copy_y(c):
        return pltpu.make_async_remote_copy(
            src_ref=part.at[c, pl.ds(other, half)],
            dst_ref=ybuf.at[c],
            send_sem=y_send.at[c],
            recv_sem=y_recv.at[c],
            device_id=dev_p,
            device_id_type=MESH,
        )

    def copy_b(c, t):
        return pltpu.make_async_remote_copy(
            src_ref=direct.at[t, c, pl.ds(mine, half)],
            dst_ref=direct.at[t, c, pl.ds(mine, half)],
            send_sem=b_send.at[c],
            recv_sem=b_recv.at[c],
            device_id=dev_p,
            device_id_type=MESH,
        )

    def copy_e(c):
        view = scal.at[c, pl.ds(pyl * NZ, NZ)]
        return pltpu.make_async_remote_copy(
            src_ref=view,
            dst_ref=view,
            send_sem=e_send.at[c],
            recv_sem=e_recv.at[c],
            device_id=dev_p,
            device_id_type=MESH,
        )

    def wait_bytes(view, sem):
        pltpu.make_async_copy(view, view, sem).wait()

    def stage_image(c, t):
        @pl.when(t > 0)
        def _():
            copy_b(c, t).wait()

        @pl.when(t == 0)
        def _():
            image(c, t, True)

        @pl.when(jnp.logical_and(t > 0, t < ROUNDS))
        def _():
            image(c, t, False)

        @pl.when(t < ROUNDS)
        def _():
            copy_y(c).start()

        @pl.when(t == ROUNDS)
        def _():
            copy_e(c).wait()
            curvature(c)
            for dz, dy in peers:
                pltpu.make_async_remote_copy(
                    src_ref=dots.at[c, item],
                    dst_ref=dots.at[c, item],
                    send_sem=d_send.at[c],
                    recv_sem=d_recv.at[c],
                    device_id=dev_z(dz, dy),
                    device_id_type=MESH,
                ).start()

    def stage_sum(c):
        copy_y(c).wait()
        zsum[c] = part[c, pl.ds(mine, half), :] + ybuf[c]
        for dz, dy in column:
            row = pl.multiple_of(place(dz, dy)[0] * piece, piece)
            pltpu.make_async_remote_copy(
                src_ref=zsum.at[c, pl.ds(row, piece)],
                dst_ref=zbuf.at[c, slot_of(dz)],
                send_sem=z_send.at[c],
                recv_sem=z_recv.at[c],
                device_id=dev_z(dz, dy),
                device_id_type=MESH,
            ).start()

    def spread(c, t):
        for dz, dy in column:
            pltpu.make_async_remote_copy(
                src_ref=direct.at[t, c, pl.ds(prow, piece)],
                dst_ref=direct.at[t, c, pl.ds(prow, piece)],
                send_sem=a_send.at[c],
                recv_sem=a_recv.at[c],
                device_id=dev_z(dz, dy),
                device_id_type=MESH,
            ).start()

    seat = pyl * NZ + pz
    lane = lax.broadcasted_iota(jnp.int32, (piece, tile), 1)
    sublane = lax.broadcasted_iota(jnp.int32, (piece, tile), 0)

    def stage_solve(c, t):
        wait_bytes(zbuf.at[c], z_send.at[c])
        wait_bytes(zbuf.at[c], z_recv.at[c])
        got = zsum[c, pl.ds(zrow, piece), :]
        for k in range(NZ - 1):
            got = got + zbuf[c, k]

        @pl.when(t == 0)
        def _():
            r = got - 1.0 * direct[0, c, pl.ds(prow, piece), :]
            rs[c] = r
            ps[c] = r
            norms[c] = jnp.broadcast_to(jnp.sum(r * r, axis=1, keepdims=True), r.shape)
            direct[1, c, pl.ds(prow, piece), :] = r

        @pl.when(t > 0)
        def _():
            p = ps[c]
            q = got + 1.0 * p
            now = norms[c]
            alpha = now / (jnp.sum(p * q, axis=1, keepdims=True) + 1e-06)
            r = rs[c] - alpha * q
            after = jnp.broadcast_to(jnp.sum(r * r, axis=1, keepdims=True), r.shape)
            p = r + after / (now + 1e-06) * p
            rs[c] = r
            ps[c] = p
            norms[c] = after
            direct[t + 1, c, pl.ds(prow, piece), :] = p
            alphas[t, c] = alpha

        spread(c, t + 1)

        @pl.when(t == ROUNDS - 1)
        def _():
            row = norms[c]
            for k in range(ITERS - 1):
                row = jnp.where(lane < (ITERS - 1 - k) * piece, alphas[ITERS - 1 - k, c], row)
            keep = jnp.logical_and(lax.rem(lane, piece) == sublane, lane < ITERS * piece)
            scal[c, seat] = jnp.sum(jnp.where(keep, row, 0.0), axis=0, keepdims=True)
            for dz, dy in column:
                pltpu.make_async_remote_copy(
                    src_ref=scal.at[c, seat],
                    dst_ref=scal.at[c, seat],
                    send_sem=s_send.at[c],
                    recv_sem=s_recv.at[c],
                    device_id=dev_z(dz, dy),
                    device_id_type=MESH,
                ).start()

    def stage_spread(c, t):
        wait_bytes(zbuf.at[c], a_send.at[c])
        wait_bytes(zbuf.at[c], a_recv.at[c])
        copy_b(c, t + 1).start()

        @pl.when(t == ROUNDS - 1)
        def _():
            view = scal.at[c, pl.ds(0, NZ - 1)]
            wait_bytes(view, s_send.at[c])
            wait_bytes(view, s_recv.at[c])
            copy_e(c).start()

    wide_lane = lax.broadcasted_iota(jnp.int32, (tile, tile), 1)
    wide_row = lax.broadcasted_iota(jnp.int32, (tile, tile), 0)

    def stage_last(c):
        rows_of = jnp.concatenate(
            [jnp.broadcast_to(scal[c, g], (piece, tile)) for g in range(NZ * NYL)], axis=0
        )

        def column_of(k):
            keep = wide_lane == lax.rem(wide_row, piece) + k * piece
            return jnp.sum(jnp.where(keep, rows_of, 0.0), axis=1, keepdims=True)

        vec = direct[ROUNDS, c]
        x = direct[0, c]
        for k in range(ITERS - 1):
            x = x + column_of(k) * direct[k + 1, c]
        norm = column_of(ITERS - 1)
        own_dot = jnp.sum(vec * vec, axis=1, keepdims=True)
        view = dots.at[c, pl.ds(0, NZ * NYL - 1)]
        wait_bytes(view, d_send.at[c])
        wait_bytes(view, d_recv.at[c])
        total = jnp.sum(dots[c], axis=0)
        total = jnp.sum(jnp.where(diagonal, total, 0.0), axis=1, keepdims=True)
        part[c] = x + norm / (total + own_dot + 1e-06) * vec
        pltpu.make_async_copy(part.at[c], out_hbm.at[c], out_sem.at[c]).start()

    def guarded(step, offset, rounds, body):
        at = step - offset
        t = lax.div(at, PERIOD)
        c = lax.rem(at, PERIOD)

        @pl.when(jnp.logical_and(at >= 0, jnp.logical_and(t < rounds, c < blocks)))
        def _():
            body(c, t)

    def step_body(step, carry):
        guarded(step, 0, ROUNDS + 1, stage_image)
        guarded(step, AT_SUM, ROUNDS, lambda c, t: stage_sum(c))
        guarded(step, AT_SOLVE, ROUNDS, stage_solve)
        guarded(step, AT_SPREAD, ROUNDS, stage_spread)

        @pl.when(step >= ROUNDS * PERIOD + AT_LAST)
        def _():
            stage_last(step - (ROUNDS * PERIOD + AT_LAST))

        return carry

    lax.fori_loop(0, ROUNDS * PERIOD + AT_LAST + blocks, step_body, 0)
    for c in range(blocks):
        pltpu.make_async_copy(part.at[c], out_hbm.at[c], out_sem.at[c]).wait()


def local(item_factors, weights, tile_ids, start_factors):
    blocks, count, tile, _ = weights.shape
    _, rows, rank = item_factors.shape
    gathered = NX * NYH * NCORE
    half = tile // NYL
    piece = half // NZ
    dma = pltpu.SemaphoreType.DMA
    vmem = pltpu.VMEM
    out = pl.pallas_call(
        functools.partial(kernel, blocks, count),
        out_shape=jax.ShapeDtypeStruct((blocks, tile, rank), F32),
        in_specs=[
            pl.BlockSpec(memory_space=pl.ANY),
            pl.BlockSpec(memory_space=pl.ANY),
            pl.BlockSpec(memory_space=pl.ANY),
            pl.BlockSpec(memory_space=pl.ANY),
        ],
        out_specs=pl.BlockSpec(memory_space=pl.ANY),
        scratch_shapes=[
            pltpu.SMEM((blocks, 1, count), jnp.int32),
            vmem((blocks * count, tile, tile), F32),
            vmem((gathered, rows, rank), F32),
            vmem((gathered * rows // tile, tile, 2 * rank), BF16),
            vmem((2 * rank, 2 * rank), F32),
            vmem((rank, 2 * rank), BF16),
            vmem((ROUNDS + 1, blocks, tile, rank), F32),
            vmem((blocks, tile, rank), F32),
            vmem((blocks, half, rank), F32),
            vmem((blocks, half, rank), F32),
            vmem((blocks, NZ - 1, piece, rank), F32),
            vmem((blocks, NZ * NYL, 1, tile), F32),
            vmem((blocks, NZ * NYL, 1, tile), F32),
            vmem((blocks, piece, rank), F32),
            vmem((blocks, piece, rank), F32),
            vmem((blocks, piece, rank), F32),
            vmem((ROUNDS, blocks, piece, rank), F32),
            dma((4,)),
            dma((blocks,)),
            dma((15 * rows // tile,)),
            dma((15 * rows // tile,)),
        ]
        + [dma((blocks,))] * 14,
        compiler_params=pltpu.CompilerParams(collective_id=0, has_side_effects=True),
        name="als_sweep",
    )(
        tile_ids,
        weights.reshape(blocks * count, tile, tile),
        item_factors.reshape(rows, rank),
        start_factors.reshape(blocks, tile, rank),
    )
    return out.reshape(blocks * tile, rank)


def solution(mesh):
    in_specs = (
        P("item", "user", None),
        P("user", "item", None, None),
        P("user", "item", None),
        P("user", None),
    )
    out_specs = P("user", None)
    return jax.shard_map(local, mesh=mesh, in_specs=in_specs, out_specs=out_specs, check_vma=False)
```

```python
import functools

import jax
import jax.numpy as jnp
from jax import lax
from jax.experimental import pallas as pl
from jax.experimental.pallas import tpu as pltpu
from jax.sharding import PartitionSpec as P

F32 = jnp.float32
BF16 = jnp.bfloat16
MESH = pl.DeviceIdType.MESH

ITERS = 3
ROUNDS = ITERS
PERIOD = 11
AT_SUM = 2
AT_SOLVE = 5
AT_SPREAD = 8
AT_LAST = 6

NX, NYH, NCORE = 4, 2, 2
NZ, NYL = 8, 2


def split(value):
    high = value.astype(BF16)
    low = (value - high.astype(F32)).astype(BF16)
    return high, low


def kernel(
    blocks,
    count,
    ids_hbm,
    weights_hbm,
    slab_hbm,
    start_hbm,
    out_hbm,
    ids_ref,
    weights_ref,
    vbuf,
    vcat,
    gram_acc,
    gram_cat,
    direct,
    part,
    ybuf,
    zsum,
    zbuf,
    scal,
    dots,
    rs,
    ps,
    norms,
    alphas,
    local_sem,
    out_sem,
    g_send,
    g_recv,
    y_send,
    y_recv,
    z_send,
    z_recv,
    a_send,
    a_recv,
    b_send,
    b_recv,
    s_send,
    s_recv,
    e_send,
    e_recv,
    d_send,
    d_recv,
):
    user = lax.axis_index("user")
    item = lax.axis_index("item")
    tile = direct.shape[2]
    half = tile // NYL
    piece = half // NZ
    rows = vbuf.shape[1]

    px, pyh, pc = user // (NYH * NCORE), lax.rem(user // NCORE, NYH), lax.rem(user, NCORE)
    pz, pyl = item // NYL, lax.rem(item, NYL)

    def uslot(x, yh, c):
        return x * (NYH * NCORE) + yh * NCORE + c

    xl, xr, xo = lax.rem(px + 3, NX), lax.rem(px + 1, NX), lax.rem(px + 2, NX)
    qyh, qc = 1 - pyh, 1 - pc
    dev_y = (uslot(px, qyh, pc), item)
    dev_l = (uslot(xl, pyh, pc), item)
    dev_r = (uslot(xr, pyh, pc), item)
    dev_o = (uslot(xo, pyh, pc), item)
    dev_c = (uslot(px, pyh, qc), item)
    dev_p = (user, pz * NYL + (1 - pyl))

    peers = [(dz, dy) for dz in (4, 3, 5, 2, 6, 1, 7, 0) for dy in (1, 0) if dz or dy]
    column = [(dz, dy) for dz, dy in peers if dy == 0]

    def place(dz, dy):
        return lax.rem(pz + dz, NZ), lax.rem(pyl + dy, NYL)

    def dev_z(dz, dy):
        z, y = place(dz, dy)
        return (user, z * NYL + y)

    def slot_of(dz):
        return column.index((NZ - dz, 0))

    zdev = {peer: dev_z(*peer) for peer in peers}
    zrows = {dz: pl.multiple_of(place(dz, 0)[0] * piece, piece) for dz, _ in column}

    barrier = pltpu.get_barrier_semaphore()
    greeted = [dev_y, dev_l, dev_r, dev_o, dev_c] + [zdev[peer] for peer in peers]
    for dev in greeted:
        pl.semaphore_signal(barrier, inc=1, device_id=dev, device_id_type=MESH)
    own = uslot(px, pyh, pc)
    load_v = pltpu.make_async_copy(slab_hbm, vbuf.at[own], local_sem.at[2])
    load_v.start()
    load_i = pltpu.make_async_copy(ids_hbm, ids_ref, local_sem.at[3])
    load_i.start()
    load_x = pltpu.make_async_copy(start_hbm, direct.at[0], local_sem.at[1])
    load_x.start()
    load_w = pltpu.make_async_copy(weights_hbm, weights_ref, local_sem.at[0])
    load_w.start()
    load_v.wait()
    pl.semaphore_wait(barrier, len(greeted))

    parts = rows // tile
    sends = []

    def send(src, slot, j, dev, kind):
        copy = pltpu.make_async_remote_copy(
            src_ref=src.at[pl.ds(j * tile, tile)],
            dst_ref=vbuf.at[slot, pl.ds(j * tile, tile)],
            send_sem=g_send.at[kind * parts + j],
            recv_sem=g_recv.at[kind * parts + j],
            device_id=dev,
            device_id_type=MESH,
        )
        copy.start()
        sends.append(copy)

    def arrived(slot, j, kind):
        view = vbuf.at[slot, pl.ds(j * tile, tile)]
        pltpu.make_async_copy(view, view, g_recv.at[kind * parts + j]).wait()

    gram_acc[...] = jnp.zeros_like(gram_acc)

    def convert(src, slot, j):
        high, low = split(src[pl.ds(j * tile, tile), :])
        cat = jnp.concatenate([high, low], axis=1)
        vcat[slot * parts + j] = cat
        gram_acc[...] += lax.dot_general(
            cat, cat, (((0,), (0,)), ((), ())), preferred_element_type=F32
        )

    Y, L0, R0, O0, L1, R1, O1, C0 = range(8)
    send(vbuf.at[own], own, 0, dev_y, Y)
    for j in (1, 0):
        send(vbuf.at[own], own, j, dev_o, O0)
        send(vbuf.at[own], own, j, dev_r, L0)
        send(vbuf.at[own], own, j, dev_l, R0)
    send(vbuf.at[own], own, 1, dev_y, Y)
    for j in range(parts):
        send(vbuf.at[own], own, j, dev_c, C0)
    for j in range(parts):
        convert(vbuf.at[own], own, j)
    across = uslot(px, qyh, pc)
    routes = [(xl, pyh, L0), (xr, pyh, R0), (xo, pyh, O0), (xl, qyh, L1), (xr, qyh, R1), (xo, qyh, O1)]

    def along(x, yh, kind):
        slot = uslot(x, yh, pc)
        arrived(slot, 1, kind)
        send(vbuf.at[slot], slot, 1, dev_y, kind + L1 - L0)
        send(vbuf.at[slot], slot, 1, dev_c, C0 + kind + 1)

    def pass_on(x, yh, kind, j):
        slot = uslot(x, yh, pc)
        arrived(slot, j, kind)
        send(vbuf.at[slot], slot, j, dev_c, C0 + kind + 1)

    along(*routes[0])
    along(*routes[1])
    arrived(across, 0, Y)
    send(vbuf.at[across], across, 0, dev_o, O1)
    send(vbuf.at[across], across, 0, dev_r, L1)
    send(vbuf.at[across], across, 0, dev_l, R1)
    send(vbuf.at[across], across, 0, dev_c, C0 + Y + 1)
    along(*routes[2])
    pass_on(px, qyh, Y, 1)
    for x, yh, kind in routes[:2]:
        pass_on(x, yh, kind, 0)
    for x, yh, kind in [(px, qyh, Y)] + routes[:2]:
        for j in range(parts):
            convert(vbuf.at[uslot(x, yh, pc)], uslot(x, yh, pc), j)
    pass_on(*routes[2], 0)
    for j in range(parts):
        convert(vbuf.at[uslot(xo, pyh, pc)], uslot(xo, pyh, pc), j)
    for x, yh, kind in [(px, pyh, -1), (px, qyh, Y)] + routes[:3]:
        for j in range(parts):
            slot = uslot(x, yh, qc)
            arrived(slot, j, C0 + kind + 1)
            convert(vbuf.at[slot], slot, j)
    for j in range(parts):
        for x, yh, kind in routes[3:]:
            pass_on(x, yh, kind, j)
    for x, yh, kind in routes[3:]:
        for j in range(parts):
            convert(vbuf.at[uslot(x, yh, pc)], uslot(x, yh, pc), j)
    for j in range(parts):
        for x, yh, kind in routes[3:]:
            slot = uslot(x, yh, qc)
            arrived(slot, j, C0 + kind + 1)
            convert(vbuf.at[slot], slot, j)
    for copy in sends:
        copy.wait_send()

    gram = gram_acc[...]
    gram = gram[:tile] + gram[tile:]
    gram = gram[:, :tile] + gram[:, tile:]
    gram_cat[...] = jnp.concatenate(split(gram), axis=1)

    load_i.wait()
    load_x.wait()
    load_w.wait()

    def operand(vec):
        high, low = split(vec)
        lhs = jnp.concatenate(
            [jnp.concatenate([high, high], axis=1), jnp.concatenate([low, low], axis=1)], axis=0
        )
        own_part = jnp.dot(
            jnp.concatenate([high, low], axis=0), gram_cat[...], preferred_element_type=F32
        )
        return lhs, own_part

    def fold(acc):
        acc = acc[:tile] + acc[tile:]
        return acc[:, :tile] + acc[:, tile:]

    def scored(lhs, c, k):
        pair = jnp.concatenate([vcat[ids_ref[c, 0, k]], vcat[ids_ref[c, 0, k + 1]]], axis=0)
        scores = lax.dot_general(lhs, pair, (((1,), (1,)), ((), ())), preferred_element_type=F32)
        base = c * count + k
        wt = jnp.concatenate([weights_ref[base], weights_ref[base + 1]], axis=1)
        return pair, scores[:tile] + scores[tile:], wt

    def image(c, t, first):
        vec = direct[t, c]
        lhs, acc = operand(-vec if first else vec)
        for k in range(0, count, 2):
            pair, scores, wt = scored(lhs, c, k)
            scaled = scores * wt
            if first:
                scaled = jnp.where(wt > 0, scaled + (1.0 + wt), 0.0)
            acc += jnp.dot(
                jnp.concatenate(split(scaled), axis=0), pair, preferred_element_type=F32
            )
        part[c] = fold(acc)

    diagonal = lax.broadcasted_iota(jnp.int32, (tile, tile), 0) == lax.broadcasted_iota(
        jnp.int32, (tile, tile), 1
    )

    def curvature(c):
        vec = direct[ROUNDS, c]
        lhs, own_part = operand(vec)
        acc = None
        for k in range(0, count, 2):
            _, scores, wt = scored(lhs, c, k)
            term = scores * scores * wt
            acc = term if acc is None else acc + term
        share = acc[:, :tile] + acc[:, tile:] + vec * fold(own_part)
        share = jnp.sum(share, axis=1, keepdims=True)
        dots[c, item] = jnp.sum(jnp.where(diagonal, share, 0.0), axis=0, keepdims=True)

    mine = pl.multiple_of(pyl * half, half)
    other = pl.multiple_of((1 - pyl) * half, half)
    zrow = pl.multiple_of(pz * piece, piece)
    prow = pl.multiple_of(pyl * half + pz * piece, piece)

    def copy_y(c):
        return pltpu.make_async_remote_copy(
            src_ref=part.at[c, pl.ds(other, half)],
            dst_ref=ybuf.at[c],
            send_sem=y_send.at[c],
            recv_sem=y_recv.at[c],
            device_id=dev_p,
            device_id_type=MESH,
        )

    def copy_b(c, t):
        return pltpu.make_async_remote_copy(
            src_ref=direct.at[t, c, pl.ds(mine, half)],
            dst_ref=direct.at[t, c, pl.ds(mine, half)],
            send_sem=b_send.at[c],
            recv_sem=b_recv.at[c],
            device_id=dev_p,
            device_id_type=MESH,
        )

    def copy_e(c):
        view = scal.at[c, pl.ds(pyl * NZ, NZ)]
        return pltpu.make_async_remote_copy(
            src_ref=view,
            dst_ref=view,
            send_sem=e_send.at[c],
            recv_sem=e_recv.at[c],
            device_id=dev_p,
            device_id_type=MESH,
        )

    def wait_bytes(view, sem):
        pltpu.make_async_copy(view, view, sem).wait()

    def stage_image(c, t):
        @pl.when(t > 0)
        def _():
            copy_b(c, t).wait()

        @pl.when(t == 0)
        def _():
            image(c, t, True)

        @pl.when(jnp.logical_and(t > 0, t < ROUNDS))
        def _():
            image(c, t, False)

        @pl.when(t < ROUNDS)
        def _():
            copy_y(c).start()

        @pl.when(t == ROUNDS)
        def _():
            copy_e(c).wait()
            curvature(c)
            for dz, dy in peers:
                pltpu.make_async_remote_copy(
                    src_ref=dots.at[c, item],
                    dst_ref=dots.at[c, item],
                    send_sem=d_send.at[c],
                    recv_sem=d_recv.at[c],
                    device_id=zdev[dz, dy],
                    device_id_type=MESH,
                ).start()

    def stage_sum(c):
        copy_y(c).wait()
        zsum[c] = part[c, pl.ds(mine, half), :] + ybuf[c]
        for dz, dy in column:
            pltpu.make_async_remote_copy(
                src_ref=zsum.at[c, pl.ds(zrows[dz], piece)],
                dst_ref=zbuf.at[c, slot_of(dz)],
                send_sem=z_send.at[c],
                recv_sem=z_recv.at[c],
                device_id=zdev[dz, dy],
                device_id_type=MESH,
            ).start()

    def spread(c, t):
        for dz, dy in column:
            pltpu.make_async_remote_copy(
                src_ref=direct.at[t, c, pl.ds(prow, piece)],
                dst_ref=direct.at[t, c, pl.ds(prow, piece)],
                send_sem=a_send.at[c],
                recv_sem=a_recv.at[c],
                device_id=zdev[dz, dy],
                device_id_type=MESH,
            ).start()

    seat = pyl * NZ + pz
    lane = lax.broadcasted_iota(jnp.int32, (piece, tile), 1)
    sublane = lax.broadcasted_iota(jnp.int32, (piece, tile), 0)

    def stage_solve(c, t):
        wait_bytes(zbuf.at[c], z_send.at[c])
        wait_bytes(zbuf.at[c], z_recv.at[c])
        got = zsum[c, pl.ds(zrow, piece), :]
        for k in range(NZ - 1):
            got = got + zbuf[c, k]

        @pl.when(t == 0)
        def _():
            r = got - 1.0 * direct[0, c, pl.ds(prow, piece), :]
            rs[c] = r
            ps[c] = r
            norms[c] = jnp.broadcast_to(jnp.sum(r * r, axis=1, keepdims=True), r.shape)
            direct[1, c, pl.ds(prow, piece), :] = r

        @pl.when(t > 0)
        def _():
            p = ps[c]
            q = got + 1.0 * p
            now = norms[c]
            alpha = now / (jnp.sum(p * q, axis=1, keepdims=True) + 1e-06)
            r = rs[c] - alpha * q
            after = jnp.broadcast_to(jnp.sum(r * r, axis=1, keepdims=True), r.shape)
            p = r + after / (now + 1e-06) * p
            rs[c] = r
            ps[c] = p
            norms[c] = after
            direct[t + 1, c, pl.ds(prow, piece), :] = p
            alphas[t, c] = alpha

        spread(c, t + 1)

        @pl.when(t == ROUNDS - 1)
        def _():
            row = norms[c]
            for k in range(ITERS - 1):
                row = jnp.where(lane < (ITERS - 1 - k) * piece, alphas[ITERS - 1 - k, c], row)
            keep = jnp.logical_and(lax.rem(lane, piece) == sublane, lane < ITERS * piece)
            scal[c, seat] = jnp.sum(jnp.where(keep, row, 0.0), axis=0, keepdims=True)
            for dz, dy in column:
                pltpu.make_async_remote_copy(
                    src_ref=scal.at[c, seat],
                    dst_ref=scal.at[c, seat],
                    send_sem=s_send.at[c],
                    recv_sem=s_recv.at[c],
                    device_id=zdev[dz, dy],
                    device_id_type=MESH,
                ).start()

    def stage_spread(c, t):
        wait_bytes(zbuf.at[c], a_send.at[c])
        wait_bytes(zbuf.at[c], a_recv.at[c])
        copy_b(c, t + 1).start()

        @pl.when(t == ROUNDS - 1)
        def _():
            view = scal.at[c, pl.ds(0, NZ - 1)]
            wait_bytes(view, s_send.at[c])
            wait_bytes(view, s_recv.at[c])
            copy_e(c).start()

    wide_lane = lax.broadcasted_iota(jnp.int32, (tile, tile), 1)
    wide_row = lax.broadcasted_iota(jnp.int32, (tile, tile), 0)

    def stage_last(c):
        rows_of = jnp.concatenate(
            [jnp.broadcast_to(scal[c, g], (piece, tile)) for g in range(NZ * NYL)], axis=0
        )

        def column_of(k):
            keep = wide_lane == lax.rem(wide_row, piece) + k * piece
            return jnp.sum(jnp.where(keep, rows_of, 0.0), axis=1, keepdims=True)

        vec = direct[ROUNDS, c]
        x = direct[0, c]
        for k in range(ITERS - 1):
            x = x + column_of(k) * direct[k + 1, c]
        norm = column_of(ITERS - 1)
        own_dot = jnp.sum(vec * vec, axis=1, keepdims=True)
        view = dots.at[c, pl.ds(0, NZ * NYL - 1)]
        wait_bytes(view, d_send.at[c])
        wait_bytes(view, d_recv.at[c])
        total = jnp.sum(dots[c], axis=0)
        total = jnp.sum(jnp.where(diagonal, total, 0.0), axis=1, keepdims=True)
        part[c] = x + norm / (total + own_dot + 1e-06) * vec
        pltpu.make_async_copy(part.at[c], out_hbm.at[c], out_sem.at[c]).start()

    def guarded(step, offset, rounds, body):
        at = step - offset
        t = lax.div(at, PERIOD)
        c = lax.rem(at, PERIOD)

        @pl.when(jnp.logical_and(at >= 0, jnp.logical_and(t < rounds, c < blocks)))
        def _():
            body(c, t)

    def step_body(step, carry):
        guarded(step, 0, ROUNDS + 1, stage_image)
        guarded(step, AT_SUM, ROUNDS, lambda c, t: stage_sum(c))
        guarded(step, AT_SOLVE, ROUNDS, stage_solve)
        guarded(step, AT_SPREAD, ROUNDS, stage_spread)

        @pl.when(step >= ROUNDS * PERIOD + AT_LAST)
        def _():
            stage_last(step - (ROUNDS * PERIOD + AT_LAST))

        return carry

    lax.fori_loop(0, ROUNDS * PERIOD + AT_LAST + blocks, step_body, 0)
    for c in range(blocks):
        pltpu.make_async_copy(part.at[c], out_hbm.at[c], out_sem.at[c]).wait()


def local(item_factors, weights, tile_ids, start_factors):
    blocks, count, tile, _ = weights.shape
    _, rows, rank = item_factors.shape
    gathered = NX * NYH * NCORE
    half = tile // NYL
    piece = half // NZ
    dma = pltpu.SemaphoreType.DMA
    vmem = pltpu.VMEM
    out = pl.pallas_call(
        functools.partial(kernel, blocks, count),
        out_shape=jax.ShapeDtypeStruct((blocks, tile, rank), F32),
        in_specs=[
            pl.BlockSpec(memory_space=pl.ANY),
            pl.BlockSpec(memory_space=pl.ANY),
            pl.BlockSpec(memory_space=pl.ANY),
            pl.BlockSpec(memory_space=pl.ANY),
        ],
        out_specs=pl.BlockSpec(memory_space=pl.ANY),
        scratch_shapes=[
            pltpu.SMEM((blocks, 1, count), jnp.int32),
            vmem((blocks * count, tile, tile), F32),
            vmem((gathered, rows, rank), F32),
            vmem((gathered * rows // tile, tile, 2 * rank), BF16),
            vmem((2 * rank, 2 * rank), F32),
            vmem((rank, 2 * rank), BF16),
            vmem((ROUNDS + 1, blocks, tile, rank), F32),
            vmem((blocks, tile, rank), F32),
            vmem((blocks, half, rank), F32),
            vmem((blocks, half, rank), F32),
            vmem((blocks, NZ - 1, piece, rank), F32),
            vmem((blocks, NZ * NYL, 1, tile), F32),
            vmem((blocks, NZ * NYL, 1, tile), F32),
            vmem((blocks, piece, rank), F32),
            vmem((blocks, piece, rank), F32),
            vmem((blocks, piece, rank), F32),
            vmem((ROUNDS, blocks, piece, rank), F32),
            dma((4,)),
            dma((blocks,)),
            dma((15 * rows // tile,)),
            dma((15 * rows // tile,)),
        ]
        + [dma((blocks,))] * 14,
        compiler_params=pltpu.CompilerParams(collective_id=0, has_side_effects=True),
        name="als_sweep",
    )(
        tile_ids,
        weights.reshape(blocks * count, tile, tile),
        item_factors.reshape(rows, rank),
        start_factors.reshape(blocks, tile, rank),
    )
    return out.reshape(blocks * tile, rank)


def solution(mesh):
    in_specs = (
        P("item", "user", None),
        P("user", "item", None, None),
        P("user", "item", None),
        P("user", None),
    )
    out_specs = P("user", None)
    return jax.shard_map(local, mesh=mesh, in_specs=in_specs, out_specs=out_specs, check_vma=False)
```
